256 devices in a mesh: gx: 16 (over y, x_lo, core), gy: 16 (over z, x_hi).
Axes of the slice: x: 4 (x_hi: 2, x_lo: 2; x = x_hi * 2 + x_lo), y: 4, z: 8, core: 2. Of those that a mesh axis runs over, the one named last changes fastest.
Arguments:
- features: bfloat16 [16, 16, 1, 96, 4096], P('gx', 'gy'), may hold values from -6 to 6
- weight: bfloat16 [96, 2592], replicated, may hold values from -0.125 to 0.125
- occupancy: int32 [16, 16, 1, 4096], P('gx', 'gy'), may hold values from 0 to 1, as said below
- adjacency: int32 [16, 16, 1, 6], P('gx', 'gy'), may hold values from -1 to 0, as said below
- cotangent: bfloat16 [16, 16, 1, 96, 4096], P('gx', 'gy'), may hold values from -6 to 6
Outputs:
- outputs: bfloat16 [16, 16, 1, 96, 4096], P('gx', 'gy')
- feature_grad: bfloat16 [16, 16, 1, 96, 4096], P('gx', 'gy')
- weight_grad: float32 [96, 2592], replicated
The draws below stay inside these ranges and needn't reach their ends.
Inputs may be any that keep to these rules, and one draw needn't show every extreme that they name: `occupancy`: 1 marks an occupied voxel; every voxel of a slot that holds no block is 0. `adjacency`: column (i, j) holds exactly one block, in slot 0 (so faces 4 and 5 are always -1). Face 0 and 1 name a slot of column (i - 1, j) and (i + 1, j), faces 2 and 3 of column (i, j - 1) and (i, j + 1), faces 4 and 5 the slots s - 1 and s + 1 of the same column; -1 where no block lies across the face or the slot is empty. The relation is symmetric.
All inputs are finite; a program needn't handle non-finite values.
Results may differ from the reference program's by a relative error of at most 0.0028.
Values may be sent and summed in bfloat16 or wider, within the bound.
No kernel may reach another device: no remote copies, remote signals or barrier semaphores. Data moves between devices by JAX's collectives and lax.ppermute only.
A program may use at most 192 MiB of HBM per device.

```python
import math
import jax
import jax.numpy as jnp
from jax import lax

C = 96
BS = 16
NB = 1
NXB = 16
NYB = 16


def block_layout(key):
    folded = jax.random.fold_in(key, 7)
    first_key, second_key = jax.random.split(folded, 2)
    bottom = jax.random.randint(first_key, (NXB, NYB), 0, 2)
    counts = jax.random.randint(second_key, (NXB, NYB), 1, NB + 1)
    bottom = bottom.at[0:2, 0].set(0)
    counts = counts.at[0:2, 0].set(NB)
    in_use = jnp.arange(NB)[None, None, :] < counts[:, :, None]
    return (bottom, counts, in_use)


def across(bottom, counts, in_use, roll_axis, offset):
    other_bottom = jnp.roll(bottom, -offset, axis=roll_axis)
    other_counts = jnp.roll(counts, -offset, axis=roll_axis)
    position = lax.broadcasted_iota(jnp.int32, bottom.shape, roll_axis) + offset
    inside = (position >= 0) & (position < bottom.shape[roll_axis])
    target = bottom[:, :, None] + jnp.arange(NB)[None, None, :] - other_bottom[:, :, None]
    present = in_use & inside[:, :, None] & (target >= 0) & (target < other_counts[:, :, None])
    return jnp.where(present, target, -1)


def draw_adjacency(key, part):
    bottom, counts, in_use = block_layout(key)
    slot_ids = jnp.broadcast_to(jnp.arange(NB)[None, None, :], in_use.shape)
    lower_slot = jnp.where(in_use & (slot_ids >= 1), slot_ids - 1, -1)
    upper_slot = jnp.where(slot_ids + 1 < counts[:, :, None], slot_ids + 1, -1)
    per_face = [across(bottom, counts, in_use, 0, -1), across(bottom, counts, in_use, 0, 1), across(bottom, counts, in_use, 1, -1), across(bottom, counts, in_use, 1, 1), lower_slot, upper_slot]
    return jnp.stack(per_face, -1).astype(jnp.int32)


def draw_occupancy(key, part):
    bottom, counts, in_use = block_layout(key)
    folded = jax.random.fold_in(key, 11)
    first_key, second_key = jax.random.split(folded, 2)
    density = jax.random.randint(first_key, (NXB, NYB, NB, 1), 2, 10)
    levels = jax.random.randint(second_key, (NXB, NYB, NB, BS ** 3), 0, 10)
    return ((levels < density) & in_use[:, :, :, None]).astype(jnp.int32)


def steps_of(rng, dims, cuts, low, top_value):
    def one(dim, parts):
        steps = jax.random.uniform(jax.random.fold_in(jax.random.fold_in(rng, 6), dim), (parts,), jnp.float32, low / len(cuts), top_value / len(cuts))
        return jnp.repeat(jnp.exp(steps), dims[dim] // parts).reshape((-1,) + (1,) * (len(dims) - dim - 1))

    gain = one(*cuts[0])
    for cut in cuts[1:]:
        gain = gain * one(*cut)
    return gain


def scatter_about(key, dims, width, bound, cuts=(), held_as=jnp.bfloat16):
    loudness = steps_of(key, dims, cuts, -0.22, 0.18) if cuts else 1.0
    result = jax.random.normal(key, dims, jnp.float32) * width * loudness
    return jnp.minimum(jnp.maximum(result, -bound), bound).astype(held_as)


def setup_inputs(seed: int = 0) -> dict:
    seeds = jax.random.split(jax.random.key(seed), 6)
    return {
        "features": scatter_about(seeds[0], (NXB, NYB, NB, C, BS**3), 1.0, 6.0, ((0, 16), (1, 16))),
        "weight": scatter_about(seeds[1], (C, 27 * C), (27 * C) ** -0.5, 0.125),
        "occupancy": draw_occupancy(jax.random.fold_in(seeds[5], 71), 0),
        "adjacency": draw_adjacency(jax.random.fold_in(seeds[5], 71), 0),
        "cotangent": scatter_about(seeds[4], (NXB, NYB, NB, C, BS**3), 1.0, 6.0, ((0, 16), (1, 16))),
    }


def shift_lower(layers, along):
    filler = jnp.zeros_like(lax.slice_in_dim(layers, 0, 1, axis=along))
    kept = lax.slice_in_dim(layers, 0, layers.shape[along] - 1, axis=along)
    return jnp.concatenate([filler, kept], along)

def shift_upper(layers, along):
    filler = jnp.zeros_like(lax.slice_in_dim(layers, 0, 1, axis=along))
    kept = lax.slice_in_dim(layers, 1, layers.shape[along], axis=along)
    return jnp.concatenate([kept, filler], along)

def select_slots(layers, slot_ids):
    chosen = jnp.zeros_like(layers)
    for source in range(layers.shape[-4]):
        matches = (slot_ids == source)[..., None, None, None]
        chosen = jnp.where(matches, layers[..., source, :, :, :][..., None, :, :, :], chosen)
    return chosen

def global_shells(values, adjacency):
    west = select_slots(shift_lower(values[..., -1, :, :], 0), adjacency[..., 0])
    east = select_slots(shift_upper(values[..., 0, :, :], 0), adjacency[..., 1])
    along_x = jnp.concatenate([west[..., None, :, :], values, east[..., None, :, :]], -3)
    south = select_slots(shift_lower(along_x[..., :, -1, :], 1), adjacency[..., 2])
    north = select_slots(shift_upper(along_x[..., :, 0, :], 1), adjacency[..., 3])
    along_y = jnp.concatenate([south[..., None, :], along_x, north[..., None, :]], -2)
    below = select_slots(along_y[..., -1], adjacency[..., 4])
    above = select_slots(along_y[..., 0], adjacency[..., 5])
    return jnp.concatenate([below[..., None], along_y, above[..., None]], -1)

def reversed_shells(values, adjacency):
    below = select_slots(values[..., -1], adjacency[..., 4])
    above = select_slots(values[..., 0], adjacency[..., 5])
    along_z = jnp.concatenate([below[..., None], values, above[..., None]], -1)
    south = select_slots(shift_lower(along_z[..., :, -1, :], 1), adjacency[..., 2])
    north = select_slots(shift_upper(along_z[..., :, 0, :], 1), adjacency[..., 3])
    along_y = jnp.concatenate([south[..., None, :], along_z, north[..., None, :]], -2)
    west = select_slots(shift_lower(along_y[..., -1, :, :], 0), adjacency[..., 0])
    east = select_slots(shift_upper(along_y[..., 0, :, :], 0), adjacency[..., 1])
    return jnp.concatenate([west[..., None, :, :], along_y, east[..., None, :, :]], -3)

def forward_and_weights(padded, gradient_masked, weight):
    blocks, channels = (padded.shape[0], padded.shape[1])
    extent = padded.shape[2] - 2
    reduced_total = jnp.zeros((blocks, channels, extent ** 3), jnp.float32)
    gathered_parts = []
    gradient_widened = gradient_masked.astype(jnp.float32)
    for along_x in range(3):
        for along_y in range(3):
            stacked_taps = jnp.stack([padded[:, :, along_x:along_x + extent, along_y:along_y + extent, along_z:along_z + extent] for along_z in range(3)], 1)
            stacked_taps = stacked_taps.reshape(blocks, 3 * channels, extent ** 3).astype(jnp.float32)
            offset = (along_x * 3 + along_y) * 3 * channels
            column_stack = weight[:, offset:offset + 3 * channels].astype(jnp.float32)
            reduced_total = reduced_total + jnp.einsum('xr,arm->axm', column_stack, stacked_taps, precision=lax.Precision.HIGHEST)
            gathered_parts.append(jnp.einsum('wyp,wep->ye', gradient_widened, stacked_taps, precision=lax.Precision.HIGHEST))
    return (reduced_total, jnp.concatenate(gathered_parts, 1))

def spread_back(grad_padded, weight):
    blocks, channels = (grad_padded.shape[0], grad_padded.shape[1])
    extent = grad_padded.shape[2] - 2
    reduced_total = jnp.zeros((blocks, channels, extent ** 3), jnp.float32)
    for along_x in range(3):
        for along_y in range(3):
            stacked_taps = jnp.stack([grad_padded[:, :, 2 - along_x:2 - along_x + extent, 2 - along_y:2 - along_y + extent, 2 - along_z:2 - along_z + extent] for along_z in range(3)], 1)
            stacked_taps = stacked_taps.reshape(blocks, 3, channels, extent ** 3).astype(jnp.float32)
            offset = (along_x * 3 + along_y) * 3 * channels
            column_stack = weight[:, offset:offset + 3 * channels].reshape(channels, 3, channels).astype(jnp.float32)
            reduced_total = reduced_total + jnp.einsum('ocj,ncov->njv', column_stack, stacked_taps, precision=lax.Precision.HIGHEST)
    return reduced_total

def reference(features, weight, occupancy, adjacency, cotangent):
    block_shape = (NXB, NYB, NB, C, BS, BS, BS)
    occupied = occupancy.astype(jnp.bfloat16)[:, :, :, None, :]
    masked = features * occupied
    gradient_masked = cotangent * occupied
    padded = global_shells(masked.reshape(block_shape), adjacency)
    grad_padded = reversed_shells(gradient_masked.reshape(block_shape), adjacency)
    wide_shape = (NXB * NYB, NB, C, BS + 2, BS + 2, BS + 2)
    padded_all = padded.reshape(wide_shape)
    grad_padded_all = grad_padded.reshape(wide_shape)
    gradient_every_block = gradient_masked.reshape((NXB * NYB, NB, C, BS ** 3))
    mask_all = occupancy.reshape((NXB * NYB, NB, 1, BS ** 3))

    def one_column(running, inputs):
        padded_block, grad_block, wide_block, mask_block = inputs
        occupied_f = mask_block.astype(jnp.float32)
        reduced_total, partial_value = forward_and_weights(padded_block, grad_block, weight)
        spread = spread_back(wide_block, weight)
        outputs = (reduced_total * occupied_f).astype(jnp.bfloat16)
        feature_grad = (spread * occupied_f).astype(jnp.bfloat16)
        return (running + partial_value, (outputs, feature_grad))
    start = jnp.zeros((C, 27 * C), jnp.float32)
    summed_grad, (outputs, feature_grad) = lax.scan(one_column, start, (padded_all, gradient_every_block, grad_padded_all, mask_all))
    scale = 1.0 / math.sqrt(NXB * NYB * NB * BS ** 3)
    weight_grad = summed_grad * scale
    out_shape = (NXB, NYB, NB, C, BS ** 3)
    return (outputs.reshape(out_shape), feature_grad.reshape(out_shape), weight_grad)
```

```python
import math

import jax
import jax.numpy as jnp
from jax import lax
from jax.experimental import pallas as pl
from jax.experimental.pallas import tpu as pltpu
from jax.sharding import PartitionSpec as P

BS = 16
PLANE = BS * BS
VOX = BS**3
C = 96
F32 = jnp.float32
BF16 = jnp.bfloat16
VMEM = pl.BlockSpec(memory_space=pltpu.VMEM)
LIMIT = pltpu.CompilerParams(vmem_limit_bytes=48 << 20)


def shifted(array, axis, by):
    size = lax.axis_size(axis)
    pairs = [(i, i + by) for i in range(size) if 0 <= i + by < size]
    return lax.ppermute(array, axis, pairs)


def swap(array, axis, mask):
    return lax.ppermute(array, axis, [(i, i ^ mask) for i in range(lax.axis_size(axis))])


def y_face(values, first):
    return jnp.concatenate(
        [values[:, x * PLANE + first : x * PLANE + first + BS] for x in range(BS)], 1
    )


def prepare_kernel(feat, cot, occ, f_out, g_out, f_south, f_north, g_south, g_north):
    occupied = occ[...].astype(BF16)
    for source, out, low, high in (
        (feat, f_out, f_south, f_north),
        (cot, g_out, g_south, g_north),
    ):
        masked = source[...] * occupied
        out[...] = masked
        low[...] = y_face(masked, 0)
        high[...] = y_face(masked, PLANE - BS)


def prepare(features, cotangent, occupancy):
    whole = jax.ShapeDtypeStruct((C, VOX), BF16)
    face = jax.ShapeDtypeStruct((C, PLANE), BF16)
    return pl.pallas_call(
        prepare_kernel,
        out_shape=(whole, whole, face, face, face, face),
        in_specs=[VMEM] * 3,
        out_specs=(VMEM,) * 6,
        compiler_params=LIMIT,
        cost_estimate=pl.CostEstimate(flops=2**20, bytes_accessed=4 << 20, transcendentals=0),
    )(features, cotangent, occupancy)


def build_shifts(centre, west, east, south, north, shifts):
    shifts[1, :, :PLANE] = west[...]
    shifts[1, :, PLANE : PLANE + VOX] = centre[...]
    shifts[1, :, PLANE + VOX :] = east[...]
    for x in range(BS + 2):
        at = slice(x * PLANE, (x + 1) * PLANE)
        plane = shifts[1, :, at]
        low = south[:, x * BS : (x + 1) * BS]
        high = north[:, x * BS : (x + 1) * BS]
        shifts[0, :, at] = jnp.concatenate([low, plane[:, : PLANE - BS]], 1)
        shifts[2, :, at] = jnp.concatenate([plane[:, BS:], high], 1)


def columns(shifts, first, width):
    pieces = []
    for a in range(3):
        for b in range(3):
            start = first + a * PLANE
            pieces.append(shifts[b, :, start : start + width])
    return jnp.concatenate(pieces, 0)


def conv_kernel(centre, west, east, south, north, mat, occ, out, shifts):
    build_shifts(centre, west, east, south, north, shifts)
    width = 1024
    z = lax.broadcasted_iota(jnp.int32, (1, width), 1) % BS
    for first in range(0, VOX, width):
        spread = jnp.dot(mat[...], columns(shifts, first, width), preferred_element_type=F32)
        low = pltpu.roll(spread[:C], 1, 1)
        high = pltpu.roll(spread[2 * C :], width - 1, 1)
        total = spread[C : 2 * C] + jnp.where(z > 0, low, 0.0) + jnp.where(z < BS - 1, high, 0.0)
        here = occ[:, first : first + width].astype(F32)
        out[:, first : first + width] = (total * here).astype(BF16)


def conv(centre, west, east, south, north, mat, occupancy):
    return pl.pallas_call(
        conv_kernel,
        out_shape=jax.ShapeDtypeStruct((C, VOX), BF16),
        in_specs=[VMEM] * 7,
        out_specs=VMEM,
        scratch_shapes=[pltpu.VMEM((3, C, VOX + 2 * PLANE), BF16)],
        compiler_params=LIMIT,
        cost_estimate=pl.CostEstimate(
            flops=2 * C * 27 * C * VOX * 2, bytes_accessed=4 << 20, transcendentals=0
        ),
    )(centre, west, east, south, north, mat, occupancy)


ROWS = 2048
LANES = 128


def weights_kernel(centre, west, east, south, north, grad, out, shifts, acc):
    build_shifts(centre, west, east, south, north, shifts)
    width = 1024
    z = lax.broadcasted_iota(jnp.int32, (1, width), 1) % BS
    for first in range(0, VOX, width):
        here = grad[:, first : first + width].astype(F32)
        up = jnp.where(z < BS - 1, pltpu.roll(here, width - 1, 1), 0.0)
        down = jnp.where(z > 0, pltpu.roll(here, 1, 1), 0.0)
        stacked = jnp.concatenate([up, here, down], 0).astype(BF16)
        part = lax.dot_general(
            stacked,
            columns(shifts, first, width),
            (((1,), (1,)), ((), ())),
            preferred_element_type=F32,
        )
        if first == 0:
            acc[:, : 9 * C] = part
            acc[:, 9 * C :] = jnp.zeros((3 * C, 7 * LANES - 9 * C), F32)
        else:
            acc[:, : 9 * C] += part
    for tile in range(7):
        out[tile * 3 * C : (tile + 1) * 3 * C, :] = acc[:, tile * LANES : (tile + 1) * LANES]
    out[7 * 3 * C :, :] = jnp.zeros((ROWS - 21 * C, LANES), F32)


def weight_partial(centre, west, east, south, north, grad):
    return pl.pallas_call(
        weights_kernel,
        out_shape=jax.ShapeDtypeStruct((ROWS, LANES), F32),
        in_specs=[VMEM] * 6,
        out_specs=VMEM,
        scratch_shapes=[
            pltpu.VMEM((3, C, VOX + 2 * PLANE), BF16),
            pltpu.VMEM((3 * C, 7 * LANES), F32),
        ],
        compiler_params=LIMIT,
        cost_estimate=pl.CostEstimate(
            flops=2 * C * 27 * C * VOX * 2, bytes_accessed=4 << 20, transcendentals=0
        ),
    )(centre, west, east, south, north, grad)


def sum_everywhere(part):
    gx = lax.axis_index("gx")
    core, chip = gx % 2, gx // 2
    low, high = part[: ROWS // 2], part[ROWS // 2 :]
    mine = jnp.where(core == 0, low, high)
    theirs = jnp.where(core == 0, high, low)
    total = mine + swap(theirs, "gx", 1)
    total = total.reshape(8, LANES, LANES)

    def slot(index):
        return lax.dynamic_index_in_dim(total, index, 0, keepdims=False)

    got = [swap(slot(chip ^ k).astype(BF16), "gx", 2 * k) for k in range(1, 8)]
    own = slot(chip)
    for piece in got:
        own = own + piece.astype(F32)
    for step in (1, 4):
        got = [swap(own, "gy", step * k) for k in (1, 2, 3)]
        own = (own + got[0]) + (got[1] + got[2])
    own = own.astype(BF16)
    got = [own] + [swap(own, "gx", 2 * k) for k in range(1, 8)]
    half = jnp.zeros((8, LANES, LANES), BF16)
    for k in range(8):
        half = lax.dynamic_update_index_in_dim(half, got[k], chip ^ k, 0)
    half = half.reshape(ROWS // 2, LANES)
    other = swap(half, "gx", 1)
    low = jnp.where(core == 0, half, other)
    high = jnp.where(core == 0, other, half)
    return jnp.concatenate([low, high], 0)


def body(features, weight, occupancy, adjacency, cotangent):
    occupancy = occupancy.reshape(1, VOX)
    near = adjacency.reshape(6) == 0
    features = features.reshape(C, VOX)
    cotangent = cotangent.reshape(C, VOX)
    f, g, f_low, f_high, g_low, g_high = prepare(features, cotangent, occupancy)

    def kept(layer, face):
        return jnp.where(near[face], layer, jnp.zeros_like(layer))

    west = kept(shifted(f[:, VOX - PLANE :], "gx", 1), 0)
    east = kept(shifted(f[:, :PLANE], "gx", -1), 1)
    edge = PLANE - BS
    send_high = jnp.concatenate([west[:, edge:], f_high, east[:, edge:]], 1)
    send_low = jnp.concatenate([west[:, :BS], f_low, east[:, :BS]], 1)
    south = kept(shifted(send_high, "gy", 1), 2)
    north = kept(shifted(send_low, "gy", -1), 3)

    part = weight_partial(f, west, east, south, north, g)
    summed = sum_everywhere(part)

    taps = weight.reshape(C, 9, 3, C)
    mat = taps.transpose(2, 0, 1, 3).reshape(3 * C, 9 * C)
    outputs = conv(f, west, east, south, north, mat, occupancy)

    g_south = kept(shifted(g_high, "gy", 1), 2)
    g_north = kept(shifted(g_low, "gy", -1), 3)
    send_high = jnp.concatenate([g_south[:, edge:], g[:, VOX - PLANE :], g_north[:, edge:]], 1)
    send_low = jnp.concatenate([g_south[:, :BS], g[:, :PLANE], g_north[:, :BS]], 1)
    g_west = kept(shifted(send_high, "gx", 1), 0)
    g_east = kept(shifted(send_low, "gx", -1), 1)
    last = PLANE + BS
    g_south = jnp.concatenate([g_west[:, :BS], g_south, g_east[:, :BS]], 1)
    g_north = jnp.concatenate([g_west[:, last:], g_north, g_east[:, last:]], 1)
    back = taps[:, ::-1, ::-1].transpose(2, 3, 1, 0).reshape(3 * C, 9 * C)
    feature_grad = conv(
        g, g_west[:, BS:last], g_east[:, BS:last], g_south, g_north, back, occupancy
    )

    slot_count = lax.axis_size("gx") * lax.axis_size("gy") * VOX
    scale = 1.0 / math.sqrt(slot_count)
    tiles = summed[: 21 * C].reshape(7, 3, C, LANES).astype(F32) * scale
    wide = tiles.transpose(2, 1, 0, 3).reshape(C, 3, 7 * LANES)[:, :, : 9 * C]
    weight_grad = wide.reshape(C, 3, 9, C).transpose(0, 2, 1, 3).reshape(C, 27 * C)
    out_shape = (1, 1, 1, C, VOX)
    return (outputs.reshape(out_shape), feature_grad.reshape(out_shape), weight_grad)


def solution(mesh):
    placed = (
        P("gx", "gy", None, None, None),
        P(),
        P("gx", "gy", None, None),
        P("gx", "gy", None, None),
        P("gx", "gy", None, None, None),
    )
    return jax.shard_map(
        body,
        mesh=mesh,
        in_specs=placed,
        out_specs=(P("gx", "gy", None, None, None), P("gx", "gy", None, None, None), P()),
        check_vma=False,
    )
```

```python
import math

import jax
import jax.numpy as jnp
from jax import lax
from jax.experimental import pallas as pl
from jax.experimental.pallas import tpu as pltpu
from jax.sharding import PartitionSpec as P

BS = 16
PLANE = BS * BS
VOX = BS**3
C = 96
F32 = jnp.float32
BF16 = jnp.bfloat16
ROWS = 2048
HALF = ROWS // 2
LANES = 128
PIECES = 6
VMEM = pl.BlockSpec(memory_space=pltpu.VMEM)
SMEM = pl.BlockSpec(memory_space=pltpu.SMEM)
HBM = pl.BlockSpec(memory_space=pltpu.HBM)
LIMIT = pltpu.CompilerParams(vmem_limit_bytes=40 << 20)


def cost(flops, moved):
    return pl.CostEstimate(flops=flops, bytes_accessed=moved, transcendentals=0)


def shifted(array, axis, by):
    size = lax.axis_size(axis)
    pairs = [(i, i + by) for i in range(size) if 0 <= i + by < size]
    return lax.ppermute(array, axis, pairs)


def swap(array, axis, mask):
    return lax.ppermute(array, axis, [(i, i ^ mask) for i in range(lax.axis_size(axis))])


def start_all(sources, targets, sems):
    copies = [
        pltpu.make_async_copy(source, target, sems.at[i])
        for i, (source, target) in enumerate(zip(sources, targets))
    ]
    for copy in copies:
        copy.start()
    return copies


def kept(layer, flag):
    return jnp.where(flag == 0, layer, jnp.zeros_like(layer))


def y_face(values, first):
    return jnp.concatenate(
        [values[:, x * PLANE + first : x * PLANE + first + BS] for x in range(BS)], 1
    )


def prepare_kernel(
    facts, feat, cot, occ, f_out, g_out, mask, x_low, x_high, y_low, y_high, f_in, g_in, occ_in, sems
):
    rows = C // PIECES
    cuts = [slice(i * rows, (i + 1) * rows) for i in range(PIECES)]
    copies = start_all(
        [occ] + [feat.at[c] for c in cuts] + [cot.at[c] for c in cuts],
        [occ_in] + [f_in.at[c] for c in cuts] + [g_in.at[c] for c in cuts],
        sems,
    )
    copies[0].wait()
    occupied = occ_in[...].astype(BF16)
    mask[...] = occ_in[...].astype(F32)
    last, edge = VOX - PLANE, PLANE - BS
    for part, source, out in ((0, f_in, f_out), (1, g_in, g_out)):
        for copy in copies[1 + part * PIECES : 1 + (part + 1) * PIECES]:
            copy.wait()
        masked = source[...] * occupied
        out[...] = masked
        to = slice(part * C, (part + 1) * C)
        low, high = masked[:, :PLANE], masked[:, last:]
        for message, plane in ((x_low, low), (x_high, high)):
            message[to, :PLANE] = plane
            edges = [kept(plane[:, :BS], facts[2]), kept(plane[:, edge:], facts[3])]
            message[to, PLANE:] = jnp.concatenate(edges, 1)
        y_low[to, :PLANE] = y_face(masked, 0)
        edges = [kept(low[:, :BS], facts[0]), kept(high[:, :BS], facts[1])]
        y_low[to, PLANE:] = jnp.concatenate(edges, 1)
        y_high[to] = y_face(masked, edge)


def prepare(facts, features, cotangent, occupancy):
    whole = jax.ShapeDtypeStruct((C, VOX), BF16)
    face = jax.ShapeDtypeStruct((2 * C, PLANE + 2 * BS), BF16)
    return pl.pallas_call(
        prepare_kernel,
        out_shape=(
            whole,
            whole,
            jax.ShapeDtypeStruct((1, VOX), F32),
            face,
            face,
            face,
            jax.ShapeDtypeStruct((2 * C, PLANE), BF16),
        ),
        in_specs=[SMEM, HBM, HBM, HBM],
        out_specs=(VMEM,) * 7,
        scratch_shapes=[
            pltpu.VMEM((C, VOX), BF16),
            pltpu.VMEM((C, VOX), BF16),
            pltpu.VMEM((1, VOX), jnp.int32),
            pltpu.SemaphoreType.DMA((1 + 2 * PIECES,)),
        ],
        compiler_params=LIMIT,
        cost_estimate=cost(2**20, 3 << 20),
    )(facts, *[pltpu.with_memory_space_constraint(x, pltpu.HBM) for x in (features, cotangent, occupancy)])


def matrices_kernel(weight, mat, back, held, sems):
    start_all([weight], [held], sems)[0].wait()
    for ab in range(9):
        for c in range(3):
            k = ab * 3 + c
            block = held[:, k * C : (k + 1) * C]
            mat[c * C : (c + 1) * C, ab * C : (ab + 1) * C] = block
            turned = block.astype(F32).T.astype(BF16)
            back[(2 - c) * C : (3 - c) * C, (8 - ab) * C : (9 - ab) * C] = turned


def matrices(weight):
    shape = jax.ShapeDtypeStruct((3 * C, 9 * C), BF16)
    return pl.pallas_call(
        matrices_kernel,
        out_shape=(shape, shape),
        in_specs=[HBM],
        out_specs=(VMEM, VMEM),
        scratch_shapes=[pltpu.VMEM((C, 27 * C), BF16), pltpu.SemaphoreType.DMA((1,))],
        compiler_params=LIMIT,
        cost_estimate=cost(2**28, 6 << 20),
    )(pltpu.with_memory_space_constraint(weight, pltpu.HBM))


def build_shifts(centre, west, east, south, north, shifts):
    shifts[1, :, :PLANE] = west
    shifts[1, :, PLANE : PLANE + VOX] = centre[...]
    shifts[1, :, PLANE + VOX :] = east
    for x in range(BS + 2):
        at = slice(x * PLANE, (x + 1) * PLANE)
        plane = shifts[1, :, at]
        shifts[0, :, at] = jnp.concatenate([south(x), plane[:, : PLANE - BS]], 1)
        shifts[2, :, at] = jnp.concatenate([plane[:, BS:], north(x)], 1)


def columns(shifts, first, width):
    pieces = []
    for a in range(3):
        for b in range(3):
            start = first + a * PLANE
            pieces.append(shifts[b, :, start : start + width])
    return jnp.concatenate(pieces, 0)


def conv_kernel(part, facts, centre, halo, from_south, from_north, mat, mask, out, south, north, shifts, sems):
    for copy in start_all([from_south, from_north], [south, north], sems):
        copy.wait()
    rows = slice(part * C, (part + 1) * C)
    if part == 0:
        pairs = [kept(south[rows, PLANE:], facts[2]), kept(north[rows], facts[3])]
    else:
        pairs = [south[rows, PLANE:], north[rows]]
    ends = [[pair[:, :BS], pair[:, BS:]] for pair in pairs]
    if part == 1:
        ends = [[kept(low, facts[0]), kept(high, facts[1])] for low, high in ends]
    faces = [kept(south[rows, :PLANE], facts[2]), halo[3 * part + 2]]

    def strip(side):
        def row(x):
            if x == 0:
                return ends[side][0]
            if x == BS + 1:
                return ends[side][1]
            return faces[side][:, (x - 1) * BS : x * BS]

        return row

    build_shifts(centre, halo[3 * part], halo[3 * part + 1], strip(0), strip(1), shifts)
    width = 1024
    z = lax.broadcasted_iota(jnp.int32, (1, width), 1) % BS
    for first in range(0, VOX, width):
        spread = jnp.dot(mat[...], columns(shifts, first, width), preferred_element_type=F32)
        low = pltpu.roll(spread[:C], 1, 1)
        high = pltpu.roll(spread[2 * C :], width - 1, 1)
        total = spread[C : 2 * C] + jnp.where(z > 0, low, 0.0) + jnp.where(z < BS - 1, high, 0.0)
        out[:, first : first + width] = (total * mask[:, first : first + width]).astype(BF16)


def conv(part, facts, centre, halo, from_south, from_north, mat, mask):
    def kernel(*refs):
        conv_kernel(part, *refs)

    return pl.pallas_call(
        kernel,
        out_shape=jax.ShapeDtypeStruct((C, VOX), BF16),
        in_specs=[SMEM, VMEM, VMEM, HBM, HBM, VMEM, VMEM],
        out_specs=VMEM,
        scratch_shapes=[
            pltpu.VMEM((2 * C, PLANE + 2 * BS), BF16),
            pltpu.VMEM((2 * C, 2 * BS), BF16),
            pltpu.VMEM((3, C, VOX + 2 * PLANE), BF16),
            pltpu.SemaphoreType.DMA((2,)),
        ],
        compiler_params=LIMIT,
        cost_estimate=cost(2 * C * 27 * C * VOX * 2, 4 << 20),
        name="conv_back" if part else "conv_out",
    )(facts, centre, halo, from_south, from_north, mat, mask)


def z_stack(values):
    wide = values.astype(F32)
    width = values.shape[1]
    z = lax.broadcasted_iota(jnp.int32, (1, width), 1) % BS
    up = jnp.where(z < BS - 1, pltpu.roll(wide, width - 1, 1), 0.0)
    down = jnp.where(z > 0, pltpu.roll(wide, 1, 1), 0.0)
    return jnp.concatenate([up, wide, down], 0).astype(BF16)


def over_voxels(left, right):
    return lax.dot_general(left, right, (((1,), (1,)), ((), ())), preferred_element_type=F32)


def inner_kernel(f, g, acc, shifts):
    nothing = jnp.zeros((C, PLANE), BF16)

    def row(x):
        return nothing[:, :BS]

    build_shifts(f, nothing, nothing, row, row, shifts)
    width = 1024
    for first in range(0, VOX, width):
        part = over_voxels(
            z_stack(g[:, first : first + width]), columns(shifts, first, width)
        )
        if first == 0:
            acc[:, : 9 * C] = part
            acc[:, 9 * C :] = jnp.zeros((3 * C, 7 * LANES - 9 * C), F32)
        else:
            acc[:, : 9 * C] += part


def inner_partial(f, g):
    return pl.pallas_call(
        inner_kernel,
        out_shape=jax.ShapeDtypeStruct((3 * C, 7 * LANES), F32),
        in_specs=[VMEM, VMEM],
        out_specs=VMEM,
        scratch_shapes=[pltpu.VMEM((3, C, VOX + 2 * PLANE), BF16)],
        compiler_params=LIMIT,
        cost_estimate=cost(2 * C * 27 * C * VOX * 2, 4 << 20),
    )(f, g)


def weights_kernel(
    facts,
    f,
    g,
    inner,
    y_high,
    from_west,
    from_east,
    from_north,
    mine,
    theirs,
    halo,
    to_north,
    to_south,
    x_in,
    y_in,
    acc,
    flat,
    sems,
):
    copies = start_all(
        [from_west, from_east, from_north],
        [x_in.at[0], x_in.at[1], y_in],
        sems,
    )
    acc[...] = inner[...]
    for copy in copies:
        copy.wait()
    edge, last = PLANE - BS, VOX - PLANE
    for part in range(2):
        rows = slice(part * C, (part + 1) * C)
        for side in range(2):
            halo[3 * part + side] = kept(x_in[side, rows, :PLANE], facts[side])
        halo[3 * part + 2] = kept(y_in[rows, :PLANE], facts[3])
    west, east, north, g_north = halo[0], halo[1], halo[2], halo[5]
    at_low, at_high = slice(PLANE, PLANE + BS), slice(PLANE + BS, PLANE + 2 * BS)
    to_north[:, :PLANE] = y_high[...]
    to_north[:C, PLANE:] = jnp.concatenate([west[:, edge:], east[:, edge:]], 1)
    to_south[:C] = jnp.concatenate([west[:, :BS], east[:, :BS]], 1)
    to_north[C:, PLANE:] = jnp.concatenate([x_in[0, C:, at_high], x_in[1, C:, at_high]], 1)
    to_south[C:] = jnp.concatenate([x_in[0, C:, at_low], x_in[1, C:, at_low]], 1)

    def add(ab, left, right):
        acc[:, ab * C : (ab + 1) * C] += over_voxels(left, right)

    gap = jnp.zeros((C, BS), BF16)
    for a, plane, at in ((0, west, 0), (2, east, last)):
        left = z_stack(g[:, at : at + PLANE])
        moved = [
            jnp.concatenate([gap, plane[:, :edge]], 1),
            plane,
            jnp.concatenate([plane[:, BS:], gap], 1),
        ]
        part = over_voxels(left, jnp.concatenate(moved, 0))
        acc[:, 3 * a * C : 3 * (a + 1) * C] += part
    left = z_stack(y_high[C:])
    moved = [jnp.concatenate([gap, north[:, :edge]], 1), north, jnp.concatenate([north[:, BS:], gap], 1)]
    part = over_voxels(left, jnp.concatenate(moved, 0))
    for a in range(3):
        ab = 3 * a + 2
        acc[:, ab * C : (ab + 1) * C] += part[:, a * C : (a + 1) * C]
    left = z_stack(g_north)
    top = y_high[:C]
    moved = [
        jnp.concatenate([west[:, edge:], top[:, :edge]], 1),
        top,
        jnp.concatenate([top[:, BS:], east[:, edge:]], 1),
    ]
    part = over_voxels(left, jnp.concatenate(moved, 0))
    for a in range(3):
        ab = 3 * a
        acc[:, ab * C : (ab + 1) * C] += part[:, a * C : (a + 1) * C]
    for ab, g_edge, f_edge in (
        (2, x_in[1, C:, at_high], y_in[:C, at_high]),
        (8, x_in[0, C:, at_high], y_in[:C, at_low]),
    ):
        add(ab, z_stack(widen(g_edge)), widen(f_edge))
    for tile in range(7):
        flat[tile * 3 * C : (tile + 1) * 3 * C] = acc[:, tile * LANES : (tile + 1) * LANES]
    flat[21 * C :] = jnp.zeros((ROWS - 21 * C, LANES), F32)
    core = facts[6]
    mine[...] = flat[pl.ds(pl.multiple_of(core * HALF, HALF), HALF)]
    theirs[...] = flat[pl.ds(pl.multiple_of((1 - core) * HALF, HALF), HALF)]


def widen(values):
    return jnp.concatenate([values, jnp.zeros((C, LANES - BS), values.dtype)], 1)


def weight_partial(facts, f, g, inner, y_high, from_west, from_east, from_north):
    half = jax.ShapeDtypeStruct((HALF, LANES), F32)
    face = jax.ShapeDtypeStruct((2 * C, PLANE + 2 * BS), BF16)
    relay = jax.ShapeDtypeStruct((2 * C, 2 * BS), BF16)
    return pl.pallas_call(
        weights_kernel,
        out_shape=(half, half, jax.ShapeDtypeStruct((6, C, PLANE), BF16), face, relay),
        in_specs=[SMEM, VMEM, VMEM, VMEM, VMEM, HBM, HBM, HBM],
        out_specs=(VMEM,) * 5,
        scratch_shapes=[
            pltpu.VMEM((2, 2 * C, PLANE + 2 * BS), BF16),
            pltpu.VMEM((2 * C, PLANE + 2 * BS), BF16),
            pltpu.VMEM((3 * C, 7 * LANES), F32),
            pltpu.VMEM((ROWS, LANES), F32),
            pltpu.SemaphoreType.DMA((3,)),
        ],
        compiler_params=LIMIT,
        cost_estimate=cost(2**28, 4 << 20),
    )(facts, f, g, inner, y_high, from_west, from_east, from_north)


def core_groups():
    return [list(range(core, lax.axis_size("gx"), 2)) for core in range(2)]


def scatter_sum(total):
    total = total.reshape(-1, LANES, LANES)
    got = lax.all_to_all(total.astype(BF16), "gx", 0, 0, axis_index_groups=core_groups())
    return got.astype(F32).sum(0)


def gather_sum(own):
    parts = lax.axis_size("gx") // 2
    own = jnp.broadcast_to(own.astype(BF16)[None], (parts, LANES, LANES))
    got = lax.all_to_all(own, "gx", 0, 0, axis_index_groups=core_groups())
    return got.reshape(HALF, LANES)


def make_result(facts, half, other, scale):
    def kernel(facts, half, other, out, flat):
        core = facts[6]
        flat[pl.ds(pl.multiple_of(core * HALF, HALF), HALF)] = half[...].astype(F32)
        flat[pl.ds(pl.multiple_of((1 - core) * HALF, HALF), HALF)] = other[...].astype(F32)
        wide = []
        for c in range(3):
            tiles = [flat[(t * 3 + c) * C : (t * 3 + c + 1) * C] * scale for t in range(7)]
            wide.append(jnp.concatenate(tiles, 1))
        blocks = [wide[c][:, ab * C : (ab + 1) * C] for ab in range(9) for c in range(3)]
        out[...] = jnp.concatenate(blocks, 1)

    return pl.pallas_call(
        kernel,
        out_shape=jax.ShapeDtypeStruct((C, 27 * C), F32),
        in_specs=[SMEM, VMEM, VMEM],
        out_specs=VMEM,
        scratch_shapes=[pltpu.VMEM((ROWS, LANES), F32)],
        compiler_params=LIMIT,
        cost_estimate=cost(2**20, 2 << 20),
    )(facts, half, other)


def body(features, weight, occupancy, adjacency, cotangent):
    occupancy = occupancy.reshape(1, VOX)
    core = lax.axis_index("gx") % 2
    facts = jnp.concatenate([adjacency.reshape(6), jnp.full((2,), core, jnp.int32)])
    features = features.reshape(C, VOX)
    cotangent = cotangent.reshape(C, VOX)
    f, g, mask, x_low, x_high, y_low, y_high = prepare(facts, features, cotangent, occupancy)
    from_north = shifted(y_low, "gy", -1)
    from_west = shifted(x_high, "gx", 1)
    from_east = shifted(x_low, "gx", -1)
    inner = inner_partial(f, g)
    mine, theirs, halo, to_north, to_south = weight_partial(
        facts, f, g, inner, y_high, from_west, from_east, from_north
    )
    got, weight = lax.optimization_barrier((swap(theirs, "gx", 1), weight))
    own = scatter_sum(mine + got)
    mat, back = matrices(weight)
    own, mat, back, to_north = lax.optimization_barrier((own, mat, back, to_north))
    from_south = shifted(to_north, "gy", 1)
    step = 1
    while step < lax.axis_size("gy"):
        own = own + swap(own, "gy", step)
        if step == 1:
            own, to_south = lax.optimization_barrier((own, to_south))
            corner_north = shifted(to_south, "gy", -1)
        step = 2 * step
    outputs = conv(0, facts, f, halo, from_south, corner_north, mat, mask)
    own, outputs = lax.optimization_barrier((own, outputs))
    half = gather_sum(own)
    feature_grad = conv(1, facts, g, halo, from_south, corner_north, back, mask)
    half, feature_grad = lax.optimization_barrier((half, feature_grad))

    slot_count = lax.axis_size("gx") * lax.axis_size("gy") * VOX
    weight_grad = make_result(facts, half, swap(half, "gx", 1), 1.0 / math.sqrt(slot_count))
    out_shape = (1, 1, 1, C, VOX)
    return (outputs.reshape(out_shape), feature_grad.reshape(out_shape), weight_grad)


def solution(mesh):
    placed = (
        P("gx", "gy", None, None, None),
        P(),
        P("gx", "gy", None, None),
        P("gx", "gy", None, None),
        P("gx", "gy", None, None, None),
    )
    return jax.shard_map(
        body,
        mesh=mesh,
        in_specs=placed,
        out_specs=(P("gx", "gy", None, None, None), P("gx", "gy", None, None, None), P()),
        check_vma=False,
    )
```

```python
import math

import jax
import jax.numpy as jnp
from jax import lax
from jax.experimental import pallas as pl
from jax.experimental.pallas import tpu as pltpu
from jax.sharding import PartitionSpec as P

BS = 16
PLANE = BS * BS
VOX = BS**3
C = 96
F32 = jnp.float32
BF16 = jnp.bfloat16
ROWS = 2048
HALF = ROWS // 2
LANES = 128
PIECES = 6
VMEM = pl.BlockSpec(memory_space=pltpu.VMEM)
SMEM = pl.BlockSpec(memory_space=pltpu.SMEM)
HBM = pl.BlockSpec(memory_space=pltpu.HBM)
LIMIT = pltpu.CompilerParams(vmem_limit_bytes=40 << 20)


def cost(flops, moved):
    return pl.CostEstimate(flops=flops, bytes_accessed=moved, transcendentals=0)


def shifted(array, axis, by):
    size = lax.axis_size(axis)
    pairs = [(i, i + by) for i in range(size) if 0 <= i + by < size]
    return lax.ppermute(array, axis, pairs)


def swap(array, axis, mask):
    return lax.ppermute(array, axis, [(i, i ^ mask) for i in range(lax.axis_size(axis))])


def start_all(sources, targets, sems):
    copies = [
        pltpu.make_async_copy(source, target, sems.at[i])
        for i, (source, target) in enumerate(zip(sources, targets))
    ]
    for copy in copies:
        copy.start()
    return copies


def kept(layer, flag):
    return jnp.where(flag == 0, layer, jnp.zeros_like(layer))


def y_face(values, first):
    return jnp.concatenate(
        [values[:, x * PLANE + first : x * PLANE + first + BS] for x in range(BS)], 1
    )


def pack_message(message, faces, *edges):
    message[: 2 * C, :] = faces
    gap = jnp.zeros((BS, PLANE - 2 * C), BF16)
    for k, each in enumerate(edges):
        pieces = [each[i * BS : (i + 1) * BS] for i in range(C // BS)]
        first = 2 * C + k * BS
        message[first : first + BS, :] = jnp.concatenate(pieces + [gap], 1)


def unpack_edges(message, k=0):
    rows = message[2 * C + k * BS : 2 * C + (k + 1) * BS, :]
    return jnp.concatenate([rows[:, 2 * BS * i : 2 * BS * (i + 1)] for i in range(C // BS)], 0)


MESSAGE = (2 * C + BS, PLANE)
RELAY = (2 * C + 2 * BS, PLANE)


def prepare_kernel(
    links, feat, cot, occ, f_out, g_out, mask, y_low, x_edges, f_in, g_in, occ_in, facts, sems
):
    rows = C // PIECES
    cuts = [slice(i * rows, (i + 1) * rows) for i in range(PIECES)]
    copies = start_all(
        [occ, links] + [feat.at[c] for c in cuts] + [cot.at[c] for c in cuts],
        [occ_in, facts] + [f_in.at[c] for c in cuts] + [g_in.at[c] for c in cuts],
        sems,
    )
    copies[0].wait()
    copies[1].wait()
    occupied = occ_in[...].astype(BF16)
    mask[...] = occ_in[...].astype(F32)
    for part, source, out in ((0, f_in, f_out), (1, g_in, g_out)):
        for copy in copies[2 + part * PIECES : 2 + (part + 1) * PIECES]:
            copy.wait()
        out[...] = source[...] * occupied
    faces = jnp.concatenate([y_face(f_out, 0), y_face(g_out, 0)], 0)
    last = VOX - PLANE
    edges = [kept(f_out[:, :BS], facts[0, 0]), kept(f_out[:, last : last + BS], facts[0, 1])]
    pack_message(y_low, faces, jnp.concatenate(edges, 1))
    for side, first in ((0, 0), (1, last)):
        low = kept(g_out[:, first : first + BS], facts[0, 2])
        high = kept(g_out[:, first + PLANE - BS : first + PLANE], facts[0, 3])
        x_edges[side] = jnp.concatenate([low, high], 1)


def prepare(facts, features, cotangent, occupancy):
    whole = jax.ShapeDtypeStruct((C, VOX), BF16)
    inputs = [pltpu.with_memory_space_constraint(x, pltpu.HBM) for x in (facts, features, cotangent, occupancy)]
    return pl.pallas_call(
        prepare_kernel,
        out_shape=(
            whole,
            whole,
            jax.ShapeDtypeStruct((1, VOX), F32),
            jax.ShapeDtypeStruct(MESSAGE, BF16),
            jax.ShapeDtypeStruct((2, C, 2 * BS), BF16),
        ),
        in_specs=[HBM] * 4,
        out_specs=(VMEM,) * 5,
        scratch_shapes=[
            pltpu.VMEM((C, VOX), BF16),
            pltpu.VMEM((C, VOX), BF16),
            pltpu.VMEM((1, VOX), jnp.int32),
            pltpu.SMEM((1, 6), jnp.int32),
            pltpu.SemaphoreType.DMA((2 + 2 * PIECES,)),
        ],
        compiler_params=LIMIT,
        cost_estimate=cost(2**20, 3 << 20),
    )(*inputs)


def faces_kernel(f, g, x_edges, x_low, x_high, y_high):
    edge = PLANE - BS
    for side, message, first in ((0, x_low, 0), (1, x_high, VOX - PLANE)):
        at = slice(first, first + PLANE)
        pack_message(message, jnp.concatenate([f[:, at], g[:, at]], 0), x_edges[side])
    y_high[:C] = y_face(f, edge)
    y_high[C:] = y_face(g, edge)


def other_faces(f, g, x_edges):
    message = jax.ShapeDtypeStruct(MESSAGE, BF16)
    return pl.pallas_call(
        faces_kernel,
        out_shape=(message, message, jax.ShapeDtypeStruct((2 * C, PLANE), BF16)),
        in_specs=[VMEM] * 3,
        out_specs=(VMEM,) * 3,
        compiler_params=LIMIT,
        cost_estimate=cost(2**20, 1 << 20),
    )(f, g, x_edges)


def matrix(back, weight):
    def kernel(weight, mat, held, sems):
        start_all([weight], [held], sems)[0].wait()
        for ab in range(9):
            for c in range(3):
                k = ab * 3 + c
                block = held[:, k * C : (k + 1) * C]
                if back:
                    turned = block.astype(F32).T.astype(BF16)
                    mat[(2 - c) * C : (3 - c) * C, (8 - ab) * C : (9 - ab) * C] = turned
                else:
                    mat[c * C : (c + 1) * C, ab * C : (ab + 1) * C] = block

    return pl.pallas_call(
        kernel,
        out_shape=jax.ShapeDtypeStruct((3 * C, 9 * C), BF16),
        in_specs=[HBM],
        out_specs=VMEM,
        scratch_shapes=[pltpu.VMEM((C, 27 * C), BF16), pltpu.SemaphoreType.DMA((1,))],
        compiler_params=LIMIT,
        cost_estimate=cost(2**28, 6 << 20),
        name="matrix_back" if back else "matrix_out",
    )(pltpu.with_memory_space_constraint(weight, pltpu.HBM))


def build_shifts(centre, west, east, south, north, shifts):
    shifts[1, :, :PLANE] = west
    shifts[1, :, PLANE : PLANE + VOX] = centre[...]
    shifts[1, :, PLANE + VOX :] = east
    for x in range(BS + 2):
        at = slice(x * PLANE, (x + 1) * PLANE)
        plane = shifts[1, :, at]
        shifts[0, :, at] = jnp.concatenate([south(x), plane[:, : PLANE - BS]], 1)
        shifts[2, :, at] = jnp.concatenate([plane[:, BS:], north(x)], 1)


def columns(shifts, first, width):
    pieces = []
    for a in range(3):
        for b in range(3):
            start = first + a * PLANE
            pieces.append(shifts[b, :, start : start + width])
    return jnp.concatenate(pieces, 0)


def conv_kernel(part, facts, centre, halo, from_south, from_north, mat, mask, out, south, north, shifts, sems):
    for copy in start_all([from_south, from_north], [south, north], sems):
        copy.wait()
    rows = slice(part * C, (part + 1) * C)
    if part == 0:
        pairs = [kept(unpack_edges(south), facts[0, 2]), kept(north[rows], facts[0, 3])]
    else:
        pairs = [unpack_edges(south, 1), north[rows]]
    ends = [[pair[:, :BS], pair[:, BS:]] for pair in pairs]
    if part == 1:
        ends = [[kept(low, facts[0, 0]), kept(high, facts[0, 1])] for low, high in ends]
    faces = [kept(south[rows], facts[0, 2]), halo[3 * part + 2]]

    def strip(side):
        def row(x):
            if x == 0:
                return ends[side][0]
            if x == BS + 1:
                return ends[side][1]
            return faces[side][:, (x - 1) * BS : x * BS]

        return row

    build_shifts(centre, halo[3 * part], halo[3 * part + 1], strip(0), strip(1), shifts)
    width = 1024
    z = lax.broadcasted_iota(jnp.int32, (1, width), 1) % BS
    for first in range(0, VOX, width):
        spread = jnp.dot(mat[...], columns(shifts, first, width), preferred_element_type=F32)
        low = pltpu.roll(spread[:C], 1, 1)
        high = pltpu.roll(spread[2 * C :], width - 1, 1)
        total = spread[C : 2 * C] + jnp.where(z > 0, low, 0.0) + jnp.where(z < BS - 1, high, 0.0)
        out[:, first : first + width] = (total * mask[:, first : first + width]).astype(BF16)


def conv(part, facts, centre, halo, from_south, from_north, mat, mask):
    def kernel(*refs):
        conv_kernel(part, *refs)

    return pl.pallas_call(
        kernel,
        out_shape=jax.ShapeDtypeStruct((C, VOX), BF16),
        in_specs=[SMEM, VMEM, VMEM, HBM, HBM, VMEM, VMEM],
        out_specs=VMEM,
        scratch_shapes=[
            pltpu.VMEM(RELAY, BF16),
            pltpu.VMEM((2 * C, 2 * BS), BF16),
            pltpu.VMEM((3, C, VOX + 2 * PLANE), BF16),
            pltpu.SemaphoreType.DMA((2,)),
        ],
        compiler_params=LIMIT,
        cost_estimate=cost(2 * C * 27 * C * VOX * 2, 4 << 20),
        name="conv_back" if part else "conv_out",
    )(facts, centre, halo, from_south, from_north, mat, mask)


def z_stack(values):
    wide = values.astype(F32)
    width = values.shape[1]
    z = lax.broadcasted_iota(jnp.int32, (1, width), 1) % BS
    up = jnp.where(z < BS - 1, pltpu.roll(wide, width - 1, 1), 0.0)
    down = jnp.where(z > 0, pltpu.roll(wide, 1, 1), 0.0)
    return jnp.concatenate([up, wide, down], 0).astype(BF16)


def over_voxels(left, right):
    return lax.dot_general(left, right, (((1,), (1,)), ((), ())), preferred_element_type=F32)


def inner_kernel(f, g, acc, shifts):
    nothing = jnp.zeros((C, PLANE), BF16)

    def row(x):
        return nothing[:, :BS]

    build_shifts(f, nothing, nothing, row, row, shifts)
    width = 1024
    for first in range(0, VOX, width):
        part = over_voxels(
            z_stack(g[:, first : first + width]), columns(shifts, first, width)
        )
        if first == 0:
            acc[:, : 9 * C] = part
            acc[:, 9 * C :] = jnp.zeros((3 * C, 7 * LANES - 9 * C), F32)
        else:
            acc[:, : 9 * C] += part


def inner_partial(f, g):
    return pl.pallas_call(
        inner_kernel,
        out_shape=jax.ShapeDtypeStruct((3 * C, 7 * LANES), F32),
        in_specs=[VMEM, VMEM],
        out_specs=VMEM,
        scratch_shapes=[pltpu.VMEM((3, C, VOX + 2 * PLANE), BF16)],
        compiler_params=LIMIT,
        cost_estimate=cost(2 * C * 27 * C * VOX * 2, 4 << 20),
    )(f, g)


def weights_kernel(
    facts,
    place,
    f,
    g,
    inner,
    y_high,
    from_west,
    from_east,
    from_north,
    mine,
    theirs,
    halo,
    to_north,
    to_south,
    x_in,
    y_in,
    acc,
    flat,
    sems,
):
    copies = start_all(
        [from_west, from_east, from_north],
        [x_in.at[0], x_in.at[1], y_in],
        sems,
    )
    acc[...] = inner[...]
    for copy in copies:
        copy.wait()
    edge, last = PLANE - BS, VOX - PLANE
    for part in range(2):
        rows = slice(part * C, (part + 1) * C)
        for side in range(2):
            halo[3 * part + side] = kept(x_in[side, rows], facts[0, side])
        halo[3 * part + 2] = kept(y_in[rows], facts[0, 3])
    west, east, north, g_north = halo[0], halo[1], halo[2], halo[5]
    on_west, on_east, on_north = [unpack_edges(m) for m in (x_in.at[0], x_in.at[1], y_in)]
    pack_message(
        to_north,
        y_high[...],
        jnp.concatenate([west[:, edge:], east[:, edge:]], 1),
        jnp.concatenate([on_west[:, BS:], on_east[:, BS:]], 1),
    )
    to_south[:C] = jnp.concatenate([west[:, :BS], east[:, :BS]], 1)
    to_south[C:] = jnp.concatenate([on_west[:, :BS], on_east[:, :BS]], 1)

    def add(ab, left, right):
        acc[:, ab * C : (ab + 1) * C] += over_voxels(left, right)

    gap = jnp.zeros((C, BS), BF16)
    for a, plane, at in ((0, west, 0), (2, east, last)):
        left = z_stack(g[:, at : at + PLANE])
        moved = [
            jnp.concatenate([gap, plane[:, :edge]], 1),
            plane,
            jnp.concatenate([plane[:, BS:], gap], 1),
        ]
        part = over_voxels(left, jnp.concatenate(moved, 0))
        acc[:, 3 * a * C : 3 * (a + 1) * C] += part
    left = z_stack(y_high[C:])
    moved = [jnp.concatenate([gap, north[:, :edge]], 1), north, jnp.concatenate([north[:, BS:], gap], 1)]
    part = over_voxels(left, jnp.concatenate(moved, 0))
    for a in range(3):
        ab = 3 * a + 2
        acc[:, ab * C : (ab + 1) * C] += part[:, a * C : (a + 1) * C]
    left = z_stack(g_north)
    top = y_high[:C]
    moved = [
        jnp.concatenate([west[:, edge:], top[:, :edge]], 1),
        top,
        jnp.concatenate([top[:, BS:], east[:, edge:]], 1),
    ]
    part = over_voxels(left, jnp.concatenate(moved, 0))
    for a in range(3):
        ab = 3 * a
        acc[:, ab * C : (ab + 1) * C] += part[:, a * C : (a + 1) * C]
    for ab, g_edge, f_edge in (
        (2, on_east[:, BS:], on_north[:, BS:]),
        (8, on_west[:, BS:], on_north[:, :BS]),
    ):
        add(ab, z_stack(widen(g_edge)), widen(f_edge))
    for tile in range(7):
        flat[tile * 3 * C : (tile + 1) * 3 * C] = acc[:, tile * LANES : (tile + 1) * LANES]
    flat[21 * C :] = jnp.zeros((ROWS - 21 * C, LANES), F32)
    core = place[0]
    mine[...] = flat[pl.ds(pl.multiple_of(core * HALF, HALF), HALF)]
    theirs[...] = flat[pl.ds(pl.multiple_of((1 - core) * HALF, HALF), HALF)]


def widen(values):
    return jnp.concatenate([values, jnp.zeros((C, LANES - BS), values.dtype)], 1)


def weight_partial(facts, place, f, g, inner, y_high, from_west, from_east, from_north):
    half = jax.ShapeDtypeStruct((HALF, LANES), F32)
    face = jax.ShapeDtypeStruct(RELAY, BF16)
    relay = jax.ShapeDtypeStruct((2 * C, 2 * BS), BF16)
    return pl.pallas_call(
        weights_kernel,
        out_shape=(half, half, jax.ShapeDtypeStruct((6, C, PLANE), BF16), face, relay),
        in_specs=[SMEM, SMEM, VMEM, VMEM, VMEM, VMEM, HBM, HBM, HBM],
        out_specs=(VMEM,) * 5,
        scratch_shapes=[
            pltpu.VMEM((2, *MESSAGE), BF16),
            pltpu.VMEM(MESSAGE, BF16),
            pltpu.VMEM((3 * C, 7 * LANES), F32),
            pltpu.VMEM((ROWS, LANES), F32),
            pltpu.SemaphoreType.DMA((3,)),
        ],
        compiler_params=LIMIT,
        cost_estimate=cost(2**28, 4 << 20),
    )(facts, place, f, g, inner, y_high, from_west, from_east, from_north)


def core_groups():
    return [list(range(core, lax.axis_size("gx"), 2)) for core in range(2)]


def scatter_sum(total):
    total = total.reshape(-1, LANES, LANES)
    got = lax.all_to_all(total.astype(BF16), "gx", 0, 0, axis_index_groups=core_groups())
    return got.astype(F32).sum(0)


def gather_sum(own):
    parts = lax.axis_size("gx") // 2
    own = jnp.broadcast_to(own.astype(BF16)[None], (parts, LANES, LANES))
    got = lax.all_to_all(own, "gx", 0, 0, axis_index_groups=core_groups())
    return got.reshape(HALF, LANES)


def make_result(place, half, other, scale):
    def kernel(place, half, other, out, flat):
        core = place[0]
        flat[pl.ds(pl.multiple_of(core * HALF, HALF), HALF)] = half[...].astype(F32)
        flat[pl.ds(pl.multiple_of((1 - core) * HALF, HALF), HALF)] = other[...].astype(F32)
        wide = []
        for c in range(3):
            tiles = [flat[(t * 3 + c) * C : (t * 3 + c + 1) * C] * scale for t in range(7)]
            wide.append(jnp.concatenate(tiles, 1))
        blocks = [wide[c][:, ab * C : (ab + 1) * C] for ab in range(9) for c in range(3)]
        out[...] = jnp.concatenate(blocks, 1)

    return pl.pallas_call(
        kernel,
        out_shape=jax.ShapeDtypeStruct((C, 27 * C), F32),
        in_specs=[SMEM, VMEM, VMEM],
        out_specs=VMEM,
        scratch_shapes=[pltpu.VMEM((ROWS, LANES), F32)],
        compiler_params=LIMIT,
        cost_estimate=cost(2**20, 2 << 20),
    )(place, half, other)


def body(features, weight, occupancy, adjacency, cotangent):
    occupancy = occupancy.reshape(1, VOX)
    place = jnp.full((1,), lax.axis_index("gx") % 2, jnp.int32)
    facts = adjacency.reshape(1, 6)
    features = features.reshape(C, VOX)
    cotangent = cotangent.reshape(C, VOX)
    f, g, mask, y_low, x_edges = prepare(facts, features, cotangent, occupancy)
    from_north = shifted(y_low, "gy", -1)
    x_low, x_high, y_high = other_faces(f, g, x_edges)
    from_west = shifted(x_high, "gx", 1)
    from_east = shifted(x_low, "gx", -1)
    inner = inner_partial(f, g)
    mine, theirs, halo, to_north, to_south = weight_partial(
        facts, place, f, g, inner, y_high, from_west, from_east, from_north
    )
    got, weight = lax.optimization_barrier((swap(theirs, "gx", 1), weight))
    own = scatter_sum(mine + got)
    mat, back = matrix(False, weight), matrix(True, weight)
    own, mat, back, to_north = lax.optimization_barrier((own, mat, back, to_north))
    from_south = shifted(to_north, "gy", 1)
    step = 1
    while step < lax.axis_size("gy"):
        own = own + swap(own, "gy", step)
        if step == 1:
            own, to_south = lax.optimization_barrier((own, to_south))
            corner_north = shifted(to_south, "gy", -1)
        step = 2 * step
    outputs = conv(0, facts, f, halo, from_south, corner_north, mat, mask)
    own, outputs = lax.optimization_barrier((own, outputs))
    half = gather_sum(own)
    feature_grad = conv(1, facts, g, halo, from_south, corner_north, back, mask)
    half, feature_grad = lax.optimization_barrier((half, feature_grad))

    slot_count = lax.axis_size("gx") * lax.axis_size("gy") * VOX
    weight_grad = make_result(place, half, swap(half, "gx", 1), 1.0 / math.sqrt(slot_count))
    out_shape = (1, 1, 1, C, VOX)
    return (outputs.reshape(out_shape), feature_grad.reshape(out_shape), weight_grad)


def solution(mesh):
    placed = (
        P("gx", "gy", None, None, None),
        P(),
        P("gx", "gy", None, None),
        P("gx", "gy", None, None),
        P("gx", "gy", None, None, None),
    )
    return jax.shard_map(
        body,
        mesh=mesh,
        in_specs=placed,
        out_specs=(P("gx", "gy", None, None, None), P("gx", "gy", None, None, None), P()),
        check_vma=False,
    )
```

```python
import math

import jax
import jax.numpy as jnp
from jax import lax
from jax.experimental import pallas as pl
from jax.experimental.pallas import tpu as pltpu
from jax.sharding import PartitionSpec as P

BS = 16
PLANE = BS * BS
VOX = BS**3
C = 96
F32 = jnp.float32
BF16 = jnp.bfloat16
ROWS = 2048
HALF = ROWS // 2
LANES = 128
PIECES = 6
VMEM = pl.BlockSpec(memory_space=pltpu.VMEM)
SMEM = pl.BlockSpec(memory_space=pltpu.SMEM)
HBM = pl.BlockSpec(memory_space=pltpu.HBM)
LIMIT = pltpu.CompilerParams(vmem_limit_bytes=40 << 20)


def cost(flops, moved):
    return pl.CostEstimate(flops=flops, bytes_accessed=moved, transcendentals=0)


def shifted(array, axis, by):
    size = lax.axis_size(axis)
    pairs = [(i, i + by) for i in range(size) if 0 <= i + by < size]
    return lax.ppermute(array, axis, pairs)


def swap(array, axis, mask):
    return lax.ppermute(array, axis, [(i, i ^ mask) for i in range(lax.axis_size(axis))])


def start_all(sources, targets, sems):
    copies = [
        pltpu.make_async_copy(source, target, sems.at[i])
        for i, (source, target) in enumerate(zip(sources, targets))
    ]
    for copy in copies:
        copy.start()
    return copies


def kept(layer, flag):
    return jnp.where(flag == 0, layer, jnp.zeros_like(layer))


def y_face(values, first):
    return jnp.concatenate(
        [values[:, x * PLANE + first : x * PLANE + first + BS] for x in range(BS)], 1
    )


def pack_message(message, faces, *edges):
    message[: 2 * C, :] = faces
    gap = jnp.zeros((BS, PLANE - 2 * C), BF16)
    for k, each in enumerate(edges):
        pieces = [each[i * BS : (i + 1) * BS] for i in range(C // BS)]
        first = 2 * C + k * BS
        message[first : first + BS, :] = jnp.concatenate(pieces + [gap], 1)


def unpack_edges(message, k=0):
    rows = message[2 * C + k * BS : 2 * C + (k + 1) * BS, :]
    return jnp.concatenate([rows[:, 2 * BS * i : 2 * BS * (i + 1)] for i in range(C // BS)], 0)


MESSAGE = (2 * C + BS, PLANE)
RELAY = (2 * C + 2 * BS, PLANE)


def prepare_kernel(
    links, feat, cot, occ, f_out, g_out, mask, y_low, x_edges, f_in, g_in, occ_in, facts, sems
):
    rows = C // PIECES
    cuts = [slice(i * rows, (i + 1) * rows) for i in range(PIECES)]
    copies = start_all(
        [occ, links] + [feat.at[c] for c in cuts] + [cot.at[c] for c in cuts],
        [occ_in, facts] + [f_in.at[c] for c in cuts] + [g_in.at[c] for c in cuts],
        sems,
    )
    copies[0].wait()
    copies[1].wait()
    occupied = occ_in[...].astype(BF16)
    mask[...] = occ_in[...].astype(F32)
    for part, source, out in ((0, f_in, f_out), (1, g_in, g_out)):
        for copy in copies[2 + part * PIECES : 2 + (part + 1) * PIECES]:
            copy.wait()
        out[...] = source[...] * occupied
    faces = jnp.concatenate([y_face(f_out, 0), y_face(g_out, 0)], 0)
    last = VOX - PLANE
    edges = [kept(f_out[:, :BS], facts[0, 0]), kept(f_out[:, last : last + BS], facts[0, 1])]
    pack_message(y_low, faces, jnp.concatenate(edges, 1))
    for side, first in ((0, 0), (1, last)):
        low = kept(g_out[:, first : first + BS], facts[0, 2])
        high = kept(g_out[:, first + PLANE - BS : first + PLANE], facts[0, 3])
        x_edges[side] = jnp.concatenate([low, high], 1)


def prepare(facts, features, cotangent, occupancy):
    whole = jax.ShapeDtypeStruct((C, VOX), BF16)
    inputs = [pltpu.with_memory_space_constraint(x, pltpu.HBM) for x in (facts, features, cotangent, occupancy)]
    return pl.pallas_call(
        prepare_kernel,
        out_shape=(
            whole,
            whole,
            jax.ShapeDtypeStruct((1, VOX), F32),
            jax.ShapeDtypeStruct(MESSAGE, BF16),
            jax.ShapeDtypeStruct((2, C, 2 * BS), BF16),
        ),
        in_specs=[HBM] * 4,
        out_specs=(VMEM,) * 5,
        scratch_shapes=[
            pltpu.VMEM((C, VOX), BF16),
            pltpu.VMEM((C, VOX), BF16),
            pltpu.VMEM((1, VOX), jnp.int32),
            pltpu.SMEM((1, 6), jnp.int32),
            pltpu.SemaphoreType.DMA((2 + 2 * PIECES,)),
        ],
        compiler_params=LIMIT,
        cost_estimate=cost(2**20, 3 << 20),
    )(*inputs)


def faces_kernel(f, g, x_edges, x_low, x_high, y_high):
    edge = PLANE - BS
    for side, message, first in ((0, x_low, 0), (1, x_high, VOX - PLANE)):
        at = slice(first, first + PLANE)
        pack_message(message, jnp.concatenate([f[:, at], g[:, at]], 0), x_edges[side])
    y_high[:C] = y_face(f, edge)
    y_high[C:] = y_face(g, edge)


def other_faces(f, g, x_edges):
    message = jax.ShapeDtypeStruct(MESSAGE, BF16)
    return pl.pallas_call(
        faces_kernel,
        out_shape=(message, message, jax.ShapeDtypeStruct((2 * C, PLANE), BF16)),
        in_specs=[VMEM] * 3,
        out_specs=(VMEM,) * 3,
        compiler_params=LIMIT,
        cost_estimate=cost(2**20, 1 << 20),
    )(f, g, x_edges)


def matrix(back, weight):
    def kernel(weight, mat, held, sems):
        start_all([weight], [held], sems)[0].wait()
        for ab in range(9):
            for c in range(3):
                k = ab * 3 + c
                block = held[:, k * C : (k + 1) * C]
                if back:
                    turned = block.astype(F32).T.astype(BF16)
                    mat[(2 - c) * C : (3 - c) * C, (8 - ab) * C : (9 - ab) * C] = turned
                else:
                    mat[c * C : (c + 1) * C, ab * C : (ab + 1) * C] = block

    return pl.pallas_call(
        kernel,
        out_shape=jax.ShapeDtypeStruct((3 * C, 9 * C), BF16),
        in_specs=[HBM],
        out_specs=VMEM,
        scratch_shapes=[pltpu.VMEM((C, 27 * C), BF16), pltpu.SemaphoreType.DMA((1,))],
        compiler_params=LIMIT,
        cost_estimate=cost(2**28, 6 << 20),
        name="matrix_back" if back else "matrix_out",
    )(pltpu.with_memory_space_constraint(weight, pltpu.HBM))


def build_shifts(centre, west, east, south, north, shifts):
    shifts[1, :, :PLANE] = west
    shifts[1, :, PLANE : PLANE + VOX] = centre[...]
    shifts[1, :, PLANE + VOX :] = east
    for x in range(BS + 2):
        at = slice(x * PLANE, (x + 1) * PLANE)
        plane = shifts[1, :, at]
        shifts[0, :, at] = jnp.concatenate([south(x), plane[:, : PLANE - BS]], 1)
        shifts[2, :, at] = jnp.concatenate([plane[:, BS:], north(x)], 1)


def columns(shifts, first, width):
    pieces = []
    for a in range(3):
        for b in range(3):
            start = first + a * PLANE
            pieces.append(shifts[b, :, start : start + width])
    return jnp.concatenate(pieces, 0)


def conv_kernel(part, facts, centre, halo, from_south, from_north, mat, mask, out, south, north, shifts, sems):
    for copy in start_all([from_south, from_north], [south, north], sems):
        copy.wait()
    rows = slice(part * C, (part + 1) * C)
    if part == 0:
        pairs = [kept(unpack_edges(south), facts[0, 2]), kept(north[rows], facts[0, 3])]
    else:
        pairs = [unpack_edges(south, 1), north[rows]]
    ends = [[pair[:, :BS], pair[:, BS:]] for pair in pairs]
    if part == 1:
        ends = [[kept(low, facts[0, 0]), kept(high, facts[0, 1])] for low, high in ends]
    faces = [kept(south[rows], facts[0, 2]), halo[3 * part + 2]]

    def strip(side):
        def row(x):
            if x == 0:
                return ends[side][0]
            if x == BS + 1:
                return ends[side][1]
            return faces[side][:, (x - 1) * BS : x * BS]

        return row

    build_shifts(centre, halo[3 * part], halo[3 * part + 1], strip(0), strip(1), shifts)
    width = 1024
    z = lax.broadcasted_iota(jnp.int32, (1, width), 1) % BS
    for first in range(0, VOX, width):
        spread = jnp.dot(mat[...], columns(shifts, first, width), preferred_element_type=F32)
        low = pltpu.roll(spread[:C], 1, 1)
        high = pltpu.roll(spread[2 * C :], width - 1, 1)
        total = spread[C : 2 * C] + jnp.where(z > 0, low, 0.0) + jnp.where(z < BS - 1, high, 0.0)
        out[:, first : first + width] = (total * mask[:, first : first + width]).astype(BF16)


def conv(part, facts, centre, halo, from_south, from_north, mat, mask):
    def kernel(*refs):
        conv_kernel(part, *refs)

    return pl.pallas_call(
        kernel,
        out_shape=jax.ShapeDtypeStruct((C, VOX), BF16),
        in_specs=[SMEM, VMEM, VMEM, HBM, HBM, VMEM, VMEM],
        out_specs=VMEM,
        scratch_shapes=[
            pltpu.VMEM(RELAY, BF16),
            pltpu.VMEM((2 * C, 2 * BS), BF16),
            pltpu.VMEM((3, C, VOX + 2 * PLANE), BF16),
            pltpu.SemaphoreType.DMA((2,)),
        ],
        compiler_params=LIMIT,
        cost_estimate=cost(2 * C * 27 * C * VOX * 2, 4 << 20),
        name="conv_back" if part else "conv_out",
    )(facts, centre, halo, from_south, from_north, mat, mask)


def z_stack(values):
    wide = values.astype(F32)
    width = values.shape[1]
    z = lax.broadcasted_iota(jnp.int32, (1, width), 1) % BS
    up = jnp.where(z < BS - 1, pltpu.roll(wide, width - 1, 1), 0.0)
    down = jnp.where(z > 0, pltpu.roll(wide, 1, 1), 0.0)
    return jnp.concatenate([up, wide, down], 0).astype(BF16)


def over_voxels(left, right):
    return lax.dot_general(left, right, (((1,), (1,)), ((), ())), preferred_element_type=F32)


def inner_kernel(f, g, acc, shifts):
    nothing = jnp.zeros((C, PLANE), BF16)

    def row(x):
        return nothing[:, :BS]

    build_shifts(f, nothing, nothing, row, row, shifts)
    width = 1024
    for first in range(0, VOX, width):
        part = over_voxels(
            z_stack(g[:, first : first + width]), columns(shifts, first, width)
        )
        if first == 0:
            acc[:, : 9 * C] = part
            acc[:, 9 * C :] = jnp.zeros((3 * C, 7 * LANES - 9 * C), F32)
        else:
            acc[:, : 9 * C] += part


def inner_partial(f, g):
    return pl.pallas_call(
        inner_kernel,
        out_shape=jax.ShapeDtypeStruct((3 * C, 7 * LANES), F32),
        in_specs=[VMEM, VMEM],
        out_specs=VMEM,
        scratch_shapes=[pltpu.VMEM((3, C, VOX + 2 * PLANE), BF16)],
        compiler_params=LIMIT,
        cost_estimate=cost(2 * C * 27 * C * VOX * 2, 4 << 20),
    )(f, g)


def weights_kernel(
    facts,
    place,
    f,
    g,
    inner,
    y_high,
    from_west,
    from_east,
    from_north,
    mine,
    theirs,
    halo,
    to_north,
    to_south,
    x_in,
    y_in,
    acc,
    sems,
):
    copies = start_all(
        [from_west, from_east, from_north],
        [x_in.at[0], x_in.at[1], y_in],
        sems,
    )
    acc[...] = inner[...]
    for copy in copies:
        copy.wait()
    edge, last = PLANE - BS, VOX - PLANE
    for part in range(2):
        rows = slice(part * C, (part + 1) * C)
        for side in range(2):
            halo[3 * part + side] = kept(x_in[side, rows], facts[0, side])
        halo[3 * part + 2] = kept(y_in[rows], facts[0, 3])
    west, east, north, g_north = halo[0], halo[1], halo[2], halo[5]
    on_west, on_east, on_north = [unpack_edges(m) for m in (x_in.at[0], x_in.at[1], y_in)]
    pack_message(
        to_north,
        y_high[...],
        jnp.concatenate([west[:, edge:], east[:, edge:]], 1),
        jnp.concatenate([on_west[:, BS:], on_east[:, BS:]], 1),
    )
    to_south[:C] = jnp.concatenate([west[:, :BS], east[:, :BS]], 1)
    to_south[C:] = jnp.concatenate([on_west[:, :BS], on_east[:, :BS]], 1)

    def add(ab, left, right):
        acc[:, ab * C : (ab + 1) * C] += over_voxels(left, right)

    gap = jnp.zeros((C, BS), BF16)
    for a, plane, at in ((0, west, 0), (2, east, last)):
        left = z_stack(g[:, at : at + PLANE])
        moved = [
            jnp.concatenate([gap, plane[:, :edge]], 1),
            plane,
            jnp.concatenate([plane[:, BS:], gap], 1),
        ]
        part = over_voxels(left, jnp.concatenate(moved, 0))
        acc[:, 3 * a * C : 3 * (a + 1) * C] += part
    left = z_stack(y_high[C:])
    moved = [jnp.concatenate([gap, north[:, :edge]], 1), north, jnp.concatenate([north[:, BS:], gap], 1)]
    part = over_voxels(left, jnp.concatenate(moved, 0))
    for a in range(3):
        ab = 3 * a + 2
        acc[:, ab * C : (ab + 1) * C] += part[:, a * C : (a + 1) * C]
    left = z_stack(g_north)
    top = y_high[:C]
    moved = [
        jnp.concatenate([west[:, edge:], top[:, :edge]], 1),
        top,
        jnp.concatenate([top[:, BS:], east[:, edge:]], 1),
    ]
    part = over_voxels(left, jnp.concatenate(moved, 0))
    for a in range(3):
        ab = 3 * a
        acc[:, ab * C : (ab + 1) * C] += part[:, a * C : (a + 1) * C]
    for ab, g_edge, f_edge in (
        (2, on_east[:, BS:], on_north[:, BS:]),
        (8, on_west[:, BS:], on_north[:, :BS]),
    ):
        add(ab, z_stack(widen(g_edge)), widen(f_edge))

    def spread(halves):
        for tile in range(7):
            start = tile * 3 * C
            for h in range(2):
                low, high = max(start, h * HALF), min(start + 3 * C, (h + 1) * HALF)
                if low < high:
                    rows = acc[low - start : high - start, tile * LANES : (tile + 1) * LANES]
                    halves[h][low - h * HALF : high - h * HALF, :] = rows
        halves[1][21 * C - HALF :, :] = jnp.zeros((ROWS - 21 * C, LANES), F32)

    @pl.when(place[0] == 0)
    def _():
        spread((mine, theirs))

    @pl.when(place[0] == 1)
    def _():
        spread((theirs, mine))


def widen(values):
    return jnp.concatenate([values, jnp.zeros((C, LANES - BS), values.dtype)], 1)


def weight_partial(facts, place, f, g, inner, y_high, from_west, from_east, from_north):
    half = jax.ShapeDtypeStruct((HALF, LANES), F32)
    face = jax.ShapeDtypeStruct(RELAY, BF16)
    relay = jax.ShapeDtypeStruct((2 * C, 2 * BS), BF16)
    return pl.pallas_call(
        weights_kernel,
        out_shape=(half, half, jax.ShapeDtypeStruct((6, C, PLANE), BF16), face, relay),
        in_specs=[SMEM, SMEM, VMEM, VMEM, VMEM, VMEM, HBM, HBM, HBM],
        out_specs=(VMEM,) * 5,
        scratch_shapes=[
            pltpu.VMEM((2, *MESSAGE), BF16),
            pltpu.VMEM(MESSAGE, BF16),
            pltpu.VMEM((3 * C, 7 * LANES), F32),
            pltpu.SemaphoreType.DMA((3,)),
        ],
        compiler_params=LIMIT,
        cost_estimate=cost(2**28, 4 << 20),
    )(facts, place, f, g, inner, y_high, from_west, from_east, from_north)


def core_groups():
    return [list(range(core, lax.axis_size("gx"), 2)) for core in range(2)]


def scatter_sum(total):
    total = total.reshape(-1, LANES, LANES)
    got = lax.all_to_all(total.astype(BF16), "gx", 0, 0, axis_index_groups=core_groups())
    return got.astype(F32).sum(0)


def gather_sum(own):
    parts = lax.axis_size("gx") // 2
    own = jnp.broadcast_to(own.astype(BF16)[None], (parts, LANES, LANES))
    got = lax.all_to_all(own, "gx", 0, 0, axis_index_groups=core_groups())
    return got.reshape(HALF, LANES)


def make_result(place, half, other, scale):
    def kernel(place, half, other, out, flat):
        core = place[0]
        flat[pl.ds(pl.multiple_of(core * HALF, HALF), HALF)] = half[...].astype(F32)
        flat[pl.ds(pl.multiple_of((1 - core) * HALF, HALF), HALF)] = other[...].astype(F32)
        wide = []
        for c in range(3):
            tiles = [flat[(t * 3 + c) * C : (t * 3 + c + 1) * C] * scale for t in range(7)]
            wide.append(jnp.concatenate(tiles, 1))
        blocks = [wide[c][:, ab * C : (ab + 1) * C] for ab in range(9) for c in range(3)]
        out[...] = jnp.concatenate(blocks, 1)

    return pl.pallas_call(
        kernel,
        out_shape=jax.ShapeDtypeStruct((C, 27 * C), F32),
        in_specs=[SMEM, VMEM, VMEM],
        out_specs=VMEM,
        scratch_shapes=[pltpu.VMEM((ROWS, LANES), F32)],
        compiler_params=LIMIT,
        cost_estimate=cost(2**20, 2 << 20),
    )(place, half, other)


def body(features, weight, occupancy, adjacency, cotangent):
    occupancy = occupancy.reshape(1, VOX)
    place = jnp.full((1,), lax.axis_index("gx") % 2, jnp.int32)
    facts = adjacency.reshape(1, 6)
    features = features.reshape(C, VOX)
    cotangent = cotangent.reshape(C, VOX)
    f, g, mask, y_low, x_edges = prepare(facts, features, cotangent, occupancy)
    from_north = shifted(y_low, "gy", -1)
    x_low, x_high, y_high = other_faces(f, g, x_edges)
    from_west = shifted(x_high, "gx", 1)
    from_east = shifted(x_low, "gx", -1)
    inner = inner_partial(f, g)
    mine, theirs, halo, to_north, to_south = weight_partial(
        facts, place, f, g, inner, y_high, from_west, from_east, from_north
    )
    got, weight = lax.optimization_barrier((swap(theirs, "gx", 1), weight))
    own = scatter_sum(mine + got)
    mat, back = matrix(False, weight), matrix(True, weight)
    own, mat, back, to_north = lax.optimization_barrier((own, mat, back, to_north))
    from_south = shifted(to_north, "gy", 1)
    step = 1
    while step < lax.axis_size("gy"):
        own = own + swap(own, "gy", step)
        if step == 1:
            own, to_south = lax.optimization_barrier((own, to_south))
            corner_north = shifted(to_south, "gy", -1)
        step = 2 * step
    outputs = conv(0, facts, f, halo, from_south, corner_north, mat, mask)
    own, outputs = lax.optimization_barrier((own, outputs))
    half = gather_sum(own)
    feature_grad = conv(1, facts, g, halo, from_south, corner_north, back, mask)
    half, feature_grad = lax.optimization_barrier((half, feature_grad))

    slot_count = lax.axis_size("gx") * lax.axis_size("gy") * VOX
    weight_grad = make_result(place, half, swap(half, "gx", 1), 1.0 / math.sqrt(slot_count))
    out_shape = (1, 1, 1, C, VOX)
    return (outputs.reshape(out_shape), feature_grad.reshape(out_shape), weight_grad)


def solution(mesh):
    placed = (
        P("gx", "gy", None, None, None),
        P(),
        P("gx", "gy", None, None),
        P("gx", "gy", None, None),
        P("gx", "gy", None, None, None),
    )
    return jax.shard_map(
        body,
        mesh=mesh,
        in_specs=placed,
        out_specs=(P("gx", "gy", None, None, None), P("gx", "gy", None, None, None), P()),
        check_vma=False,
    )
```
